32 devices in a mesh: dp: 8 (over z, y), row: 2 (over core), col: 2 (over x).
Axes of the slice: x: 2, y: 2, z: 4, core: 2. Of those that a mesh axis runs over, the one named last changes fastest.
Arguments:
- inputs: bfloat16 [4096, 2048], P(('dp', 'row'), 'col'), may hold values from -6 to 6
- gain_attn: float32 [2048], P('col'), may hold values from 0.5 to 1.5
- w_keys: bfloat16 [2048, 4096], P('col', 'row'), may hold values from -0.125 to 0.125
- w_values: bfloat16 [2048, 8224], P('col', 'row'), may hold values from -0.125 to 0.125
- conv_weight: float32 [4, 8192], P(None, 'row'), may hold values from -3 to 3
- decay_log: float32 [16], P('row'), may hold values from -4 to 0.5
- step_bias: float32 [16], P('row'), may hold values from -2 to 1
- gain_head: float32 [256], replicated, may hold values from 0.5 to 1.5
- w_out: bfloat16 [4096, 2048], P('row', 'col'), may hold values from -0.1875 to 0.1875
- gain_mlp: float32 [2048], P('col'), may hold values from 0.5 to 1.5
- w_gate: bfloat16 [2048, 5504], P('col', 'row'), may hold values from -0.125 to 0.125
- w_up: bfloat16 [2048, 5504], P('col', 'row'), may hold values from -0.125 to 0.125
- w_down: bfloat16 [5504, 2048], P('row', 'col'), may hold values from -0.109375 to 0.109375
- seq_lens: int32 [16, 3], P('dp'), may hold values from 1 to 128, 256 in all within a row
- cotangent: float32 [4096, 2048], P(('dp', 'row'), 'col'), may hold values from -6 to 6
Outputs:
- result: float32 [4096, 2048], P(('dp', 'row'), 'col')
- input_grad: float32 [4096, 2048], P(('dp', 'row'), 'col')
- grad_gain_attn: float32 [2048], P('col')
- grad_w_keys: float32 [2048, 4096], P('col', 'row')
- grad_w_values: float32 [2048, 8224], P('col', 'row')
- grad_conv: float32 [4, 8192], P(None, 'row')
- grad_decay_log: float32 [16], P('row')
- grad_step_bias: float32 [16], P('row')
- grad_gain_head: float32 [256], replicated
- grad_w_out: float32 [4096, 2048], P('row', 'col')
- grad_gain_mlp: float32 [2048], P('col')
- grad_w_gate: float32 [2048, 5504], P('col', 'row')
- grad_w_up: float32 [2048, 5504], P('col', 'row')
- grad_w_down: float32 [5504, 2048], P('row', 'col')
The draws below stay inside these ranges and needn't reach their ends.
Inputs may be any that keep to these rules, and one draw needn't show every extreme that they name: `seq_lens`: row b describes packed block b, the token rows b * 256 to (b + 1) * 256 - 1: the lengths of two documents placed in order from the block's start, then the number of padded slots after them; each row sums to 256, and its largest entry is 128.
All inputs are finite; a program needn't handle non-finite values.
Results may differ from the reference program's by a relative error of at most 0.015.
Values may be sent and summed in bfloat16 or wider, within the bound.
A program may use at most 320 MiB of HBM per device.

```python
import math
import jax
import jax.numpy as jnp
import numpy as np
from jax import lax

D = 2048
HEADS = 16
DK = 128
DV = 256
FF = 5504
KCONV = 4
BLOCK = 64
TOK_DEV = 128
TOKENS = 4096
N_DP = 8
N_ROW = 2
N_COL = 2


def block_levels(key, dims, split, least, high):
    def one(dim, parts):
        draws = jax.random.uniform(jax.random.fold_in(jax.random.fold_in(key, 6), dim), (parts,), jnp.float32, least / len(split), high / len(split))
        return jnp.repeat(jnp.exp(draws), dims[dim] // parts).reshape((-1,) + (1,) * (len(dims) - dim - 1))

    level = one(*split[0])
    for cut in split[1:]:
        level = level * one(*cut)
    return level


def split_up(number_of, total, most, slope):
    portions = [(1 << 20) // math.isqrt(standing ** slope) + 1 for standing in range(2, number_of + 1)]
    rest, given = total - most - (number_of - 1), [1] * (number_of - 1)
    while rest > 0:
        movable = [i for i in range(number_of - 1) if given[i] < most]
        pool, budget = sum([portions[i] for i in movable]), rest
        for i in movable:
            more = min(most - given[i], max(1, budget * portions[i] // pool), rest)
            given[i] = given[i] + more
            rest = rest - more
    return np.array([most] + given)


def ragged(stream_key, count, total, bound, slope):
    if count == 2:
        one = jax.random.randint(stream_key, (), max(1, total - bound), min(bound, total - 1) + 1)
        return jnp.stack([one, total - one])
    sizes = jnp.asarray(split_up(count, total, bound, slope), jnp.int32)
    twos = (count - 1) // 2
    donor, receiver = sizes[1:1 + 2 * twos:2], sizes[2:2 + 2 * twos:2]
    room = jnp.minimum(donor - 1, bound - receiver)
    shifted = jax.random.randint(jax.random.fold_in(stream_key, 1), (twos,), 0, 1 << 20) % (room + 1)
    sizes = sizes.at[1:1 + 2 * twos:2].set(donor - shifted).at[2:2 + 2 * twos:2].set(receiver + shifted)
    return sizes[jax.random.permutation(jax.random.fold_in(stream_key, 2), count)]


def centred(key, extent, width, reach, cuts=(), held_as=jnp.bfloat16):
    values = jax.random.normal(key, extent, jnp.float32) * width
    if len(cuts) > 0:
        values = block_levels(key, extent, cuts, -0.22, 0.18) * values
    return jnp.clip(values, min=-reach, max=reach).astype(held_as)


def setup_inputs(seed: int = 0) -> dict:
    streams_of = jax.random.split(jax.random.key(seed), 16)
    return {
        "inputs": centred(streams_of[0], (TOKENS, D), 1.0, 6.0, ((0, 16), (1, 2))),
        "gain_attn": jnp.clip(1.0 + 0.1 * jax.random.normal(streams_of[1], (D,), jnp.float32), 0.5, 1.5),
        "w_keys": centred(streams_of[2], (D, HEADS * 2 * DK), D ** -0.5, 0.125, ((0, 2), (1, 2))),
        "w_values": centred(streams_of[3], (D, HEADS * (2 * DV + 2)), D ** -0.5, 0.125, ((0, 2), (1, 2))),
        "conv_weight": centred(streams_of[4], (KCONV, HEADS * (2 * DK + DV)), KCONV ** -0.5, 3.0, ((1, 2),), jnp.float32),
        "decay_log": jnp.clip(-4.0 + 4.5 * jax.random.uniform(streams_of[5], (HEADS,), jnp.float32) ** block_levels(streams_of[5], (HEADS,), ((0, 2),), -0.2, 0.2), -4.0, 0.5),
        "step_bias": jnp.clip(-2.0 + 3.0 * jax.random.uniform(streams_of[6], (HEADS,), jnp.float32) ** block_levels(streams_of[6], (HEADS,), ((0, 2),), -0.2, 0.2), -2.0, 1.0),
        "gain_head": jnp.clip(1.0 + 0.1 * jax.random.normal(streams_of[7], (DV,), jnp.float32), 0.5, 1.5),
        "w_out": centred(streams_of[8], (HEADS * DV, D), (HEADS * DV // 4) ** -0.5, 0.1875, ((0, 2), (1, 2))),
        "gain_mlp": jnp.clip(1.0 + 0.1 * jax.random.normal(streams_of[9], (D,), jnp.float32), 0.5, 1.5),
        "w_gate": centred(streams_of[10], (D, FF), D ** -0.5, 0.125, ((0, 2), (1, 2))),
        "w_up": centred(streams_of[11], (D, FF), D ** -0.5, 0.125, ((0, 2), (1, 2))),
        "w_down": centred(streams_of[12], (FF, D), (FF // 2) ** -0.5, 0.109375, ((0, 2), (1, 2))),
        "seq_lens": jax.vmap(lambda own: ragged(own, 3, TOK_DEV * N_ROW, TOK_DEV * N_ROW // 2, 0))(jax.random.split(streams_of[13], (N_DP * N_COL))).reshape((N_DP * N_COL, 3)).astype(jnp.int32),
        "cotangent": centred(streams_of[14], (TOKENS, D), 1.0, 6.0, ((0, 16), (1, 2)), jnp.float32),
    }


exact_setting = lax.Precision.HIGHEST

@jax.custom_vjp
def low(v):
    return lax.optimization_barrier(v.astype(jnp.bfloat16)).astype(jnp.float32)

@jax.custom_vjp
def low_back(v):
    return v

def low_keep(v):
    return (low(v), None)

def low_pass(kept, grad):
    return (grad,)

def back_keep(v):
    return (v, None)

def back_low(kept, grad):
    return (low(grad),)
low.defvjp(low_keep, low_pass)
low_back.defvjp(back_keep, back_low)

def to_blocks(tensor, blocks):
    shaped = tensor.reshape((blocks, BLOCK) + tensor.shape[1:])
    return jnp.swapaxes(shaped, 1, 2)

def delta_mixer(keys_proj, values_proj, conv_weight, decay_log, step_bias, gain_head, segment):
    length = keys_proj.shape[0]
    head_count = keys_proj.shape[1] // (2 * DK)
    key_part = keys_proj.reshape(length, head_count, 2 * DK)
    value_part = values_proj.reshape(length, head_count, 2 * DV + 2)
    conv_in = jnp.concatenate([key_part, value_part[:, :, :DV]], axis=2).reshape(length, head_count * (2 * DK + DV))
    conv_sum = conv_weight[0][None, :] * conv_in
    for offset in range(1, KCONV):
        earlier = jnp.concatenate([jnp.zeros((offset, conv_in.shape[1]), jnp.float32), conv_in[:length - offset]], axis=0)
        earlier_seg = jnp.concatenate([jnp.full((offset,), -1, jnp.int32), segment[:length - offset]])
        same_doc = (earlier_seg == segment).astype(jnp.float32)
        conv_sum = conv_sum + conv_weight[offset][None, :] * earlier * same_doc[:, None]
    activated = jax.nn.silu(conv_sum).reshape(length, head_count, 2 * DK + DV)
    query_rows = activated[:, :, :DK]
    key_rows = activated[:, :, DK:2 * DK]
    value_rows = activated[:, :, 2 * DK:]
    query_rows = query_rows * lax.rsqrt(lax.optimization_barrier(jnp.sum(query_rows * query_rows, axis=2, keepdims=True)) + 1e-06) * DK ** (-0.5)
    key_rows = key_rows * lax.rsqrt(lax.optimization_barrier(jnp.sum(key_rows * key_rows, axis=2, keepdims=True)) + 1e-06)
    gate_raw = value_part[:, :, DV:2 * DV]
    write_rate = jax.nn.sigmoid(value_part[:, :, 2 * DV])
    log_decay = -jnp.exp(decay_log)[None, :] * jax.nn.softplus(value_part[:, :, 2 * DV + 1] + step_bias[None, :])
    blocks = length // BLOCK
    query_b = to_blocks(query_rows, blocks)
    key_b = to_blocks(key_rows, blocks)
    value_b = to_blocks(value_rows, blocks)
    rate_b = to_blocks(write_rate, blocks)
    cumulative = jnp.cumsum(to_blocks(log_decay, blocks), axis=2)
    seg_b = segment.reshape(blocks, BLOCK)
    seg_prev = jnp.concatenate([jnp.full((1,), -1, jnp.int32), seg_b[:blocks - 1, BLOCK - 1]])
    places = jnp.arange(BLOCK, dtype=jnp.int32)
    lower_mask = places[:, None] >= places[None, :]
    strict_mask = (places[:, None] > places[None, :]).astype(jnp.float32)
    keep_pair = ((seg_b[:, :, None] == seg_b[:, None, :]) & lower_mask[None])[:, None]
    log_gap = cumulative[:, :, :, None] - cumulative[:, :, None, :]
    decay_pair = jnp.where(keep_pair, jnp.exp(jnp.where(keep_pair, log_gap, 0.0)), 0.0)
    start_keep = (seg_b == seg_prev[:, None])[:, None, :]
    decay_start = jnp.where(start_keep, jnp.exp(cumulative), 0.0)
    end_keep = (seg_b == seg_b[:, BLOCK - 1:])[:, None, :]
    decay_end = jnp.where(end_keep, jnp.exp(cumulative[:, :, BLOCK - 1:] - cumulative), 0.0)
    decay_whole = decay_start[:, :, BLOCK - 1]
    key_gram = jnp.einsum('nhik,nhjk->nhij', key_b, key_b, precision=exact_setting)
    system = jnp.eye(BLOCK, dtype=jnp.float32) + key_gram * decay_pair * strict_mask * rate_b[:, :, :, None]
    right_side = jnp.concatenate([rate_b[:, :, :, None] * value_b, (rate_b * decay_start)[:, :, :, None] * key_b], axis=3)
    solved = jax.scipy.linalg.solve_triangular(system, right_side, lower=True, unit_diagonal=True)
    new_values = solved[:, :, :, :DV]
    weighted = solved[:, :, :, DV:]
    scores = jnp.einsum('nhik,nhjk->nhij', query_b, key_b, precision=exact_setting) * decay_pair

    def advance(carried_state, pieces):
        newest_portion, weighted_portion, query_fragment, key_fragment, score_part, opening_portion, ending_portion, entire_portion = pieces
        state_update = newest_portion - jnp.einsum('nlq,nqp->nlp', weighted_portion, carried_state, precision=exact_setting)
        layer_output = opening_portion[:, :, None] * jnp.einsum('nlq,nqp->nlp', query_fragment, carried_state, precision=exact_setting)
        layer_output = layer_output + jnp.einsum('hcj,hjv->hcv', score_part, state_update, precision=exact_setting)
        carried_state = entire_portion[:, None, None] * carried_state + jnp.einsum('awo,awm->aom', key_fragment * ending_portion[:, :, None], state_update, precision=exact_setting)
        return (carried_state, layer_output)
    zero_state = jnp.zeros((head_count, DK, DV), jnp.float32)
    final_state, outputs = lax.scan(advance, zero_state, (new_values, weighted, query_b, key_b, scores, decay_start, decay_end, decay_whole))
    outputs = jnp.swapaxes(outputs, 1, 2).reshape(length, head_count, DV)
    normed = outputs * lax.rsqrt(lax.optimization_barrier(jnp.mean(outputs * outputs, axis=2, keepdims=True)) + 1e-05)
    gated_out = normed * gain_head[None, None, :] * jax.nn.silu(gate_raw)
    return gated_out.reshape(length, head_count * DV)

def rms_scale(values):
    return values * lax.rsqrt(lax.optimization_barrier(jnp.mean(values * values, axis=-1, keepdims=True)) + 1e-05)

def matmul(left_mat, right_mat):
    return jnp.dot(left_mat.astype(jnp.float32), right_mat.astype(jnp.float32), precision=exact_setting, preferred_element_type=jnp.float32)

def reference(inputs, gain_attn, w_keys, w_values, conv_weight, decay_log, step_bias, gain_head, w_out, gain_mlp, w_gate, w_up, w_down, seq_lens, cotangent):
    span_rows = TOK_DEV * N_ROW
    block_count = N_DP * N_COL
    positions = jnp.arange(span_rows, dtype=jnp.int32)
    first_end = seq_lens[:, 0:1]
    doc_end = seq_lens[:, 0:1] + seq_lens[:, 1:2]
    segments = (positions[None, :] >= first_end).astype(jnp.int32) + (positions[None, :] >= doc_end).astype(jnp.int32)
    row_mask = (positions[None, :] < doc_end).astype(jnp.float32).reshape(block_count * span_rows)

    def forward(inputs, gain_attn, w_keys, w_values, conv_weight, decay_log, step_bias, gain_head, w_out, gain_mlp, w_gate, w_up, w_down):
        normed_attn = low(rms_scale(inputs) * gain_attn[None, :])
        keys_proj = low_back(matmul(normed_attn, w_keys))
        values_proj = low_back(matmul(normed_attn, w_values))

        def one_block(pieces):
            return delta_mixer(pieces[0], pieces[1], conv_weight, decay_log, step_bias, gain_head, pieces[2])
        mixed_out = lax.map(jax.checkpoint(one_block), (keys_proj.reshape(block_count, span_rows, HEADS * 2 * DK), values_proj.reshape(block_count, span_rows, HEADS * (2 * DV + 2)), segments))
        mixed_out = low(mixed_out.reshape(block_count * span_rows, HEADS * DV))
        resid_mid = inputs + low_back(matmul(mixed_out, w_out))
        normed_mlp = low(rms_scale(resid_mid) * gain_mlp[None, :])
        gate_pre = low_back(matmul(normed_mlp, w_gate))
        up_pre = low_back(matmul(normed_mlp, w_up))
        hidden = low(jax.nn.silu(gate_pre) * up_pre)
        return resid_mid + low_back(matmul(hidden, w_down))
    floats = (inputs.astype(jnp.float32), gain_attn, w_keys.astype(jnp.float32), w_values.astype(jnp.float32), conv_weight, decay_log, step_bias, gain_head, w_out.astype(jnp.float32), gain_mlp, w_gate.astype(jnp.float32), w_up.astype(jnp.float32), w_down.astype(jnp.float32))
    result, pullback = jax.vjp(forward, *floats)
    gradients = pullback(cotangent * row_mask[:, None])
    return (result, gradients[0], gradients[1], gradients[2], gradients[3], gradients[4], gradients[5], gradients[6], gradients[7], gradients[8], gradients[9], gradients[10], gradients[11], gradients[12])
```

```python
from functools import partial

import jax
import jax.numpy as jnp
from jax import lax
from jax.experimental import pallas as pl
from jax.experimental.pallas import tpu as pltpu
from jax.sharding import PartitionSpec as P

DK = 128
DV = 256
KCONV = 4
HEAD_IN = 2 * DK + DV
HEAD_VALUES = 2 * DV + 2
F32 = jnp.float32
BF16 = jnp.bfloat16

NN = (((1,), (0,)), ((), ()))
NT = (((1,), (1,)), ((), ()))
TN = (((0,), (0,)), ((), ()))


def halves(a):
    high = a.astype(BF16)
    return high, (a - high.astype(F32)).astype(BF16)


def dot3(a, b, dims=NN):
    a_high, a_low = a if isinstance(a, tuple) else halves(a)
    b_high, b_low = b if isinstance(b, tuple) else halves(b)
    left = dims[0][0][0]
    right = dims[0][1][0]
    return lax.dot_general(
        jnp.concatenate([a_high, a_high, a_low], axis=left),
        jnp.concatenate([b_high, b_low, b_high], axis=right),
        dims,
        preferred_element_type=F32,
    )


def sigmoid(v):
    return 1.0 / (1.0 + jnp.exp(-v))


def softplus(v):
    return jnp.maximum(v, 0.0) + jnp.log(1.0 + jnp.exp(-jnp.abs(v)))


def grid_ids(n):
    return (
        lax.broadcasted_iota(jnp.int32, (n, n), 0),
        lax.broadcasted_iota(jnp.int32, (n, n), 1),
    )


def head_pieces(head, pre, window, meta, conv_w, decay_log, step_bias):
    rows = pre.shape[0]
    picked = pltpu.roll(window, window.shape[1] - 2 * head, 1)
    conv_in = jnp.concatenate([pre, picked[:, :DV]], axis=1)
    gate = picked[:, DV : 2 * DV]
    rate = sigmoid(picked[:, 2 * DV : 2 * DV + 1])
    step_in = picked[:, 2 * DV + 1 : 2 * DV + 2] + step_bias
    strength = jnp.exp(jnp.full((1, 1), decay_log, F32))
    log_decay = -strength * softplus(step_in)
    conv = conv_w[0:1, :] * conv_in
    for s in range(1, KCONV):
        conv = conv + conv_w[s : s + 1, :] * (
            pltpu.roll(conv_in, s, 0) * meta[:, s : s + 1]
        )
    sig = sigmoid(conv)
    act = conv * sig
    q_act, k_act, values = act[:, :DK], act[:, DK : 2 * DK], act[:, 2 * DK :]
    q_scale = lax.rsqrt(jnp.sum(q_act * q_act, axis=1, keepdims=True) + 1e-06)
    k_scale = lax.rsqrt(jnp.sum(k_act * k_act, axis=1, keepdims=True) + 1e-06)
    query = q_act * (q_scale * DK ** (-0.5))
    key = k_act * k_scale
    row_id, col_id = grid_ids(rows)
    after = row_id > col_id
    d_high = log_decay.astype(BF16).astype(F32)
    d_mid = (log_decay - d_high).astype(BF16).astype(F32)
    d_low = log_decay - d_high - d_mid
    lower = jnp.where(row_id >= col_id, 1.0, 0.0).astype(BF16)
    terms = jnp.concatenate(
        [jnp.where(after, d, 0.0).astype(BF16) for d in (d_high, d_mid, d_low)], axis=0
    )
    gap = lax.dot_general(
        jnp.concatenate([lower, lower, lower], axis=1), terms, NN, preferred_element_type=F32
    )
    return dict(
        conv_in=conv_in, gate=gate, rate=rate, step_in=step_in, strength=strength,
        log_decay=log_decay, conv=conv, sig=sig, q_act=q_act, k_act=k_act, values=values,
        q_scale=q_scale, k_scale=k_scale, query=query, key=key, gap=gap, after=after,
        row_id=row_id, col_id=col_id,
    )


def unit_lower_inverse(strict, row_id, col_id):
    n = strict.shape[0]
    differ = row_id ^ col_id
    below = row_id > col_id
    inverse = jnp.where(row_id == col_id, 1.0, 0.0) - jnp.where(
        (differ == 1) & below, strict, 0.0
    )
    size = 2
    while size < n:
        part = jnp.where((differ >= size) & (differ < 2 * size) & below, strict, 0.0)
        split = halves(inverse)
        inverse = inverse - dot3(split, dot3(part, split))
        size *= 2
    return inverse


def pair_mask(seg_col, seg_row, row_id, col_id):
    return jnp.where((seg_col == seg_row) & (row_id >= col_id), 1.0, 0.0)


def fill_values(own_ref, other_ref, values_ref):
    width = own_ref.shape[1]
    values_ref[:, pl.ds(values_ref.shape[1] - 128, 128)] = jnp.zeros(
        (values_ref.shape[0], 128), F32
    )
    values_ref[:, :width] = own_ref[...] + other_ref[...].astype(F32)


def mixer_forward_kernel(
    decay_ref, bias_ref, pk_ref, rk_ref, pv_ref, rv_ref, meta_ref, seg_ref, conv_ref, gain_ref,
    mixed_ref, inverse_ref,
    values_ref, mask_ref,
):
    head = pl.program_id(0)
    rows = pk_ref.shape[0]

    @pl.when(head == 0)
    def _():
        fill_values(pv_ref, rv_ref, values_ref)
        row_id, col_id = grid_ids(rows)
        mask_ref[...] = pair_mask(meta_ref[:, 0:1], seg_ref[0:1, :], row_id, col_id)

    window = values_ref[:, pl.ds(pl.multiple_of(head * (2 * DV), 128), 2 * DV + 128)]
    p = head_pieces(
        head, pk_ref[...] + rk_ref[...].astype(F32), window, meta_ref[...], conv_ref[...],
        decay_ref[head], bias_ref[head],
    )
    decay_pair = jnp.exp(p["gap"]) * mask_ref[...]
    key = halves(p["key"])
    gram = dot3(key, key, NT)
    strict = jnp.where(p["after"], gram * decay_pair, 0.0) * p["rate"]
    inverse = unit_lower_inverse(strict, p["row_id"], p["col_id"])
    inverse_ref[0] = inverse
    updates = dot3(inverse, p["rate"] * p["values"])
    scores = dot3(p["query"], key, NT) * decay_pair
    out = dot3(scores, updates)
    out = out * lax.rsqrt(jnp.mean(out * out, axis=1, keepdims=True) + 1e-05)
    gate = p["gate"]
    mixed_ref[...] = (out * gain_ref[...] * (gate * sigmoid(gate))).astype(BF16)


def mixer_backward_kernel(
    decay_ref, bias_ref, pk_ref, rk_ref, pv_ref, rv_ref, meta_ref, seg_ref, conv_ref, gain_ref,
    inverse_ref, pg_ref, rg_ref,
    dk_ref, dv_ref, small_ref,
    values_ref, mask_ref, grads_ref,
):
    head = pl.program_id(0)
    rows = pk_ref.shape[0]

    @pl.when(head == 0)
    def _():
        fill_values(pv_ref, rv_ref, values_ref)
        row_id, col_id = grid_ids(rows)
        mask_ref[...] = pair_mask(meta_ref[:, 0:1], seg_ref[0:1, :], row_id, col_id)
        grads_ref[...] = jnp.zeros_like(grads_ref)

    lanes = pl.ds(pl.multiple_of(head * (2 * DV), 128), 2 * DV + 128)
    meta = meta_ref[...]
    conv_w = conv_ref[...]
    p = head_pieces(
        head, pk_ref[...] + rk_ref[...].astype(F32), values_ref[:, lanes], meta, conv_w,
        decay_ref[head], bias_ref[head],
    )
    rate, values, gate = p["rate"], p["values"], p["gate"]
    gain = gain_ref[...]
    decay_pair = jnp.exp(p["gap"]) * mask_ref[...]
    decay_strict = jnp.where(p["after"], decay_pair, 0.0)
    key, query = halves(p["key"]), halves(p["query"])
    gram = dot3(key, key, NT) * decay_strict
    inverse = halves(inverse_ref[0])
    updates = halves(dot3(inverse, rate * values))
    scores = dot3(query, key, NT) * decay_pair
    scores_split = halves(scores)
    out = dot3(scores_split, updates)
    grad = pg_ref[...] + rg_ref[...].astype(F32)
    scale = lax.rsqrt(jnp.mean(out * out, axis=1, keepdims=True) + 1e-05)
    normed = out * scale
    gate_sig = sigmoid(gate)
    gate_act = gate * gate_sig
    d_gain = jnp.sum(grad * normed * gate_act, axis=0, keepdims=True)
    d_gate = grad * normed * gain * (gate_sig * (1.0 + gate * (1.0 - gate_sig)))
    d_normed = grad * gain * gate_act
    d_out = scale * d_normed - normed * (
        scale * jnp.mean(d_normed * normed, axis=1, keepdims=True)
    )
    d_out = halves(d_out)
    d_scores = dot3(d_out, updates, NT)
    d_updates = dot3(scores_split, d_out, TN)
    d_right = dot3(inverse, d_updates, TN)
    d_strict = -dot3(d_right, updates, NT)
    d_gap = d_scores * scores + d_strict * gram * rate
    d_qk = halves(d_scores * decay_pair)
    d_gram = halves(d_strict * decay_strict * rate)
    d_query = dot3(d_qk, key)
    d_key = dot3(d_qk, query, TN) + dot3(d_gram, key) + dot3(d_gram, key, TN)
    d_rate = jnp.sum(d_strict * gram, axis=1, keepdims=True) + jnp.sum(
        d_right * values, axis=1, keepdims=True
    )
    d_values = rate * d_right
    gap_high, gap_low = halves(d_gap)
    upper = jnp.where(p["col_id"] >= p["row_id"], 1.0, 0.0).astype(BF16)
    spans = lax.dot_general(
        jnp.concatenate([upper, upper], axis=1),
        jnp.concatenate([gap_high, gap_low], axis=0),
        NN,
        preferred_element_type=F32,
    )
    d_log = jnp.sum(jnp.where(p["after"], spans, 0.0), axis=1, keepdims=True)
    d_step = -p["strength"] * d_log * sigmoid(p["step_in"])
    d_decay = jnp.sum(d_log * p["log_decay"], axis=0, keepdims=True)
    d_bias = jnp.sum(d_step, axis=0, keepdims=True)
    d_rate = d_rate * rate * (1.0 - rate)
    q_scale, k_scale = p["q_scale"], p["k_scale"]
    d_query = d_query * DK ** (-0.5)
    d_q_act = q_scale * d_query - p["q_act"] * (
        q_scale * q_scale * q_scale * jnp.sum(d_query * p["q_act"], axis=1, keepdims=True)
    )
    d_k_act = k_scale * d_key - p["k_act"] * (
        k_scale * k_scale * k_scale * jnp.sum(d_key * p["k_act"], axis=1, keepdims=True)
    )
    sig, conv, conv_in = p["sig"], p["conv"], p["conv_in"]
    d_conv = jnp.concatenate([d_q_act, d_k_act, d_values], axis=1) * (
        sig * (1.0 + conv * (1.0 - sig))
    )
    d_in = conv_w[0:1, :] * d_conv
    tap_grads = [jnp.sum(d_conv * conv_in, axis=0, keepdims=True)]
    for s in range(1, KCONV):
        masked = d_conv * meta[:, s : s + 1]
        tap_grads.append(
            jnp.sum(masked * pltpu.roll(conv_in, s, 0), axis=0, keepdims=True)
        )
        d_in = d_in + conv_w[s : s + 1, :] * pltpu.roll(masked, rows - s, 0)
    dk_ref[...] = d_in[:, : 2 * DK].astype(BF16)
    lane = lax.broadcasted_iota(jnp.int32, (rows, 128), 1)
    last = jnp.where(lane == 0, d_rate, jnp.where(lane == 1, d_step, 0.0))
    wide = jnp.concatenate([d_in[:, 2 * DK :], d_gate, last], axis=1)
    grads_ref[:, lanes] = grads_ref[:, lanes] + pltpu.roll(wide, 2 * head, 1)
    lane_row = lax.broadcasted_iota(jnp.int32, (1, HEAD_IN - DV), 1)
    ends = jnp.where(lane_row == 0, d_decay, jnp.where(lane_row == 1, d_bias, 0.0))
    small_ref[0] = jnp.concatenate(
        tap_grads
        + [jnp.concatenate([d_gain, ends], axis=1), jnp.zeros((3, HEAD_IN), F32)],
        axis=0,
    )

    @pl.when(head == pl.num_programs(0) - 1)
    def _():
        dv_ref[...] = grads_ref[:, : dv_ref.shape[1]].astype(BF16)


def mixer_specs(rows, wide):
    full = lambda shape: pl.BlockSpec(shape, lambda h: (0,) * len(shape))
    head_cols = pl.BlockSpec((rows, 2 * DK), lambda h: (0, h))
    scalars = pl.BlockSpec(memory_space=pltpu.SMEM)
    return [
        scalars, scalars, head_cols, head_cols, full((rows, wide)), full((rows, wide)),
        full((rows, 8)), full((8, rows)), pl.BlockSpec((KCONV, HEAD_IN), lambda h: (0, h)),
        full((1, DV)),
    ]


def padded_width(heads):
    return heads * 2 * DV + 128


def mixer_forward(args):
    pk, pv = args[2], args[4]
    rows, heads, wide = pk.shape[0], pk.shape[1] // (2 * DK), pv.shape[1]
    square = pl.BlockSpec((1, rows, rows), lambda h: (h, 0, 0))
    return pl.pallas_call(
        mixer_forward_kernel,
        grid=(heads,),
        in_specs=mixer_specs(rows, wide),
        out_specs=[pl.BlockSpec((rows, DV), lambda h: (0, h)), square],
        out_shape=[
            jax.ShapeDtypeStruct((rows, heads * DV), BF16),
            jax.ShapeDtypeStruct((heads, rows, rows), F32),
        ],
        scratch_shapes=[
            pltpu.VMEM((rows, padded_width(heads)), F32),
            pltpu.VMEM((rows, rows), F32),
        ],
        compiler_params=pltpu.CompilerParams(
            dimension_semantics=("arbitrary",), vmem_limit_bytes=50 * 2**20
        ),
        cost_estimate=pl.CostEstimate(
            flops=heads * 50 * 2 * rows**3, bytes_accessed=16 * 2**20, transcendentals=0
        ),
        name="mixer_forward",
    )(*args)


def mixer_backward(args, inverse, pg, rg):
    pk, pv = args[2], args[4]
    rows, heads, wide = pk.shape[0], pk.shape[1] // (2 * DK), pv.shape[1]
    square = pl.BlockSpec((1, rows, rows), lambda h: (h, 0, 0))
    head_cols = pl.BlockSpec((rows, DV), lambda h: (0, h))
    return pl.pallas_call(
        mixer_backward_kernel,
        grid=(heads,),
        in_specs=mixer_specs(rows, wide) + [square, head_cols, head_cols],
        out_specs=[
            pl.BlockSpec((rows, 2 * DK), lambda h: (0, h)),
            pl.BlockSpec((rows, wide), lambda h: (0, 0)),
            pl.BlockSpec((1, 8, HEAD_IN), lambda h: (h, 0, 0)),
        ],
        out_shape=[
            jax.ShapeDtypeStruct((rows, heads * 2 * DK), BF16),
            jax.ShapeDtypeStruct((rows, wide), BF16),
            jax.ShapeDtypeStruct((heads, 8, HEAD_IN), F32),
        ],
        scratch_shapes=[
            pltpu.VMEM((rows, padded_width(heads)), F32),
            pltpu.VMEM((rows, rows), F32),
            pltpu.VMEM((rows, padded_width(heads)), F32),
        ],
        compiler_params=pltpu.CompilerParams(
            dimension_semantics=("arbitrary",), vmem_limit_bytes=50 * 2**20
        ),
        cost_estimate=pl.CostEstimate(
            flops=heads * 50 * 2 * rows**3, bytes_accessed=20 * 2**20, transcendentals=0
        ),
        name="mixer_backward",
    )(*args, inverse, pg, rg)


def swap(value, axis):
    return lax.ppermute(value, axis, [(0, 1), (1, 0)])


def ring_order(n):
    if n == 8:
        return [0, 2, 4, 6, 7, 5, 3, 1]
    return list(range(n))


def ring_sum(parts, place, order):
    n = len(order)
    forward = [(order[i], order[(i + 1) % n]) for i in range(n)]
    backward = [(b, a) for a, b in forward]
    total = jnp.zeros(parts.shape, F32)

    def chunk(index, way):
        got = lax.dynamic_slice(parts, (index, way, 0, 0), (1, 1) + parts.shape[2:])
        return got.reshape(parts.shape[2:])

    held = [chunk(place, 0), chunk(place, 1)]
    for s in range(1, n):
        came = [lax.ppermute(held[0], "dp", forward), lax.ppermute(held[1], "dp", backward)]
        mine = [chunk((place - s) % n, 0), chunk((place + s) % n, 1)]
        held = [
            (came[w].astype(F32) + mine[w].astype(F32)).astype(BF16) for w in (0, 1)
        ]

    def put(total, value, index, way):
        return lax.dynamic_update_slice(
            total, value.astype(F32)[None, None], (index, way, 0, 0)
        )

    for s in range(n):
        total = put(total, held[0], (place + 1 - s) % n, 0)
        total = put(total, held[1], (place - 1 + s) % n, 1)
        if s < n - 1:
            held = [
                lax.ppermute(held[0], "dp", forward),
                lax.ppermute(held[1], "dp", backward),
            ]
    return total


def as_chunks(grad, n):
    return grad.reshape((n, 2, grad.shape[0] // (2 * n)) + grad.shape[1:])


def sum_groups(value, n):
    step = 1
    while step < n:
        value = value + lax.ppermute(value, "dp", [(i, i ^ step) for i in range(n)])
        step *= 2
    return value


def mm(a, b, dims=NN):
    return lax.dot_general(a, b, dims, preferred_element_type=F32)


def pair_sum(row_sums):
    return row_sums + swap(row_sums, "col")


def norm_forward(values, gain, width):
    totals = pair_sum(jnp.sum(values * values, axis=1))
    scale = lax.rsqrt(totals / width + 1e-05)
    return (values * scale[:, None] * gain[None, :]).astype(BF16), scale


def norm_backward(values, gain, scale, grad, width):
    scaled = grad * gain[None, :]
    inner = pair_sum(jnp.sum(scaled * values, axis=1))
    part = scale[:, None] * scaled - values * (scale * scale * scale * inner / width)[:, None]
    return part, jnp.sum(grad * values * scale[:, None], axis=0)


def layer(
    groups,
    inputs,
    gain_attn,
    w_keys,
    w_values,
    conv_weight,
    decay_log,
    step_bias,
    gain_head,
    w_out,
    gain_mlp,
    w_gate,
    w_up,
    w_down,
    seq_lens,
    cotangent,
):
    rows, half_width = inputs.shape
    width = 2 * half_width
    row = lax.axis_index("row")
    col = lax.axis_index("col")
    order = ring_order(groups)
    places = [0] * groups
    for i, d in enumerate(order):
        places[d] = i
    place = jnp.asarray(places, jnp.int32)[lax.axis_index("dp")]
    same = row == col

    def by_col(first, second):
        return jnp.where(same, first, second), jnp.where(same, second, first)

    ends = seq_lens[:, 0] + seq_lens[:, 1]
    positions = jnp.arange(rows, dtype=jnp.int32)
    row_mask = (positions < ends[row]).astype(F32)
    lens = seq_lens[col]
    segment = (positions >= lens[0]).astype(jnp.int32) + (
        positions >= lens[0] + lens[1]
    ).astype(jnp.int32)
    earlier = [
        ((jnp.roll(segment, s) == segment) & (positions >= s)).astype(F32)
        for s in range(1, KCONV)
    ]
    seg_f = segment.astype(F32)
    meta = jnp.stack([seg_f] + earlier + [seg_f] * (8 - KCONV), axis=1)
    seg_row = jnp.broadcast_to(seg_f[None, :], (8, rows))

    out_grad = cotangent * row_mask[:, None]
    mlp_grad_own = out_grad.astype(BF16)
    mlp_grad = jnp.concatenate([mlp_grad_own, swap(mlp_grad_own, "row")], axis=0)

    x = inputs.astype(F32)
    normed_own, scale_attn = norm_forward(x, gain_attn, width)
    normed_keep, normed_send = by_col(normed_own, swap(normed_own, "row"))
    rk = swap(mm(normed_send, w_keys).astype(BF16), "col")
    rv = swap(mm(normed_send, w_values).astype(BF16), "col")
    pk = mm(normed_keep, w_keys)
    pv = mm(normed_keep, w_values)
    mixer_args = (
        decay_log, step_bias, pk, rk, pv, rv, meta, seg_row, conv_weight, gain_head[None, :],
    )
    mixed_keep, inverse = mixer_forward(mixer_args)
    mixed_own, mixed_other = by_col(mixed_keep, swap(mixed_keep, "col"))

    hidden_part = mm(mlp_grad, w_down, NT)
    hidden_grad = hidden_part + swap(hidden_part.astype(BF16), "col").astype(F32)

    resid_mid = x + (mm(mixed_own, w_out) + swap(mm(mixed_other, w_out), "row"))

    normed_mlp_own, scale_mlp = norm_forward(resid_mid, gain_mlp, width)
    normed_mlp = jnp.concatenate([normed_mlp_own, swap(normed_mlp_own, "row")], axis=0)
    gate_part = mm(normed_mlp, w_gate)
    up_part = mm(normed_mlp, w_up)
    gate_pre = gate_part + swap(gate_part.astype(BF16), "col").astype(F32)
    up_pre = up_part + swap(up_part.astype(BF16), "col").astype(F32)
    sig = jax.nn.sigmoid(gate_pre)
    gate_act = gate_pre * sig
    hidden = (gate_act * up_pre).astype(BF16)
    gate_grad = (hidden_grad * up_pre * sig * (1.0 + gate_pre * (1.0 - sig))).astype(BF16)
    up_grad = (hidden_grad * gate_act).astype(BF16)

    normed_part = mm(gate_grad, w_gate, NT) + mm(up_grad, w_up, NT)
    normed_mlp_grad = normed_part[:rows] + swap(normed_part[rows:], "row")
    mid_grad, grad_gain_mlp = norm_backward(
        resid_mid, gain_mlp, scale_mlp, normed_mlp_grad, width
    )
    resid_grad = out_grad + mid_grad
    attn_grad_own = resid_grad.astype(BF16)
    attn_grad_other = swap(attn_grad_own, "row")
    attn_keep, attn_send = by_col(attn_grad_own, attn_grad_other)
    rg = swap(mm(attn_send, w_out, NT).astype(BF16), "col")
    pg = mm(attn_keep, w_out, NT)

    down_part = mm(hidden, w_down)
    result = resid_mid + (down_part[:rows] + swap(down_part[rows:], "row"))

    step = 16 * groups
    units = hidden.shape[1]
    padded = jnp.pad(hidden, ((0, 0), (0, -units % step)))
    grad_w_down = mm(padded, mlp_grad, TN).astype(BF16)
    grad_w_gate = mm(normed_mlp, gate_grad, TN).astype(BF16)
    grad_w_up = mm(normed_mlp, up_grad, TN).astype(BF16)
    mixed_rows = jnp.concatenate([mixed_own, mixed_other], axis=0)
    attn_rows = jnp.concatenate([attn_grad_own, attn_grad_other], axis=0)
    grad_w_out = mm(mixed_rows, attn_rows, TN).astype(BF16)

    def reduced(grad):
        total = ring_sum(as_chunks(grad, groups), place, order)
        return total.reshape(grad.shape)

    grad_w_down = reduced(grad_w_down)[:units]
    grad_w_gate = reduced(grad_w_gate)
    grad_w_up = reduced(grad_w_up)
    grad_w_out = reduced(grad_w_out)

    dk_keep, dv_keep, small = mixer_backward(mixer_args, inverse, pg, rg)
    dk_send, dv_send = swap(dk_keep, "col"), swap(dv_keep, "col")
    normed_rows = jnp.concatenate([normed_keep, normed_send], axis=0)
    dk = jnp.concatenate([dk_keep, dk_send], axis=0)
    dv = jnp.concatenate([dv_keep, dv_send], axis=0)
    grad_w_keys = reduced(mm(normed_rows, dk, TN).astype(BF16))
    grad_w_values = reduced(mm(normed_rows, dv, TN).astype(BF16))
    back = mm(dk, w_keys, NT) + mm(dv, w_values, NT)
    back_own, back_other = by_col(back[:rows], back[rows:])
    normed_attn_grad = back_own + swap(back_other, "row")
    input_part, grad_gain_attn = norm_backward(
        x, gain_attn, scale_attn, normed_attn_grad, width
    )
    input_grad = resid_grad + input_part

    heads = small.shape[0]
    taps = small[:, :KCONV]
    others = small[:, KCONV]
    gain_row = jnp.pad(jnp.sum(others[:, :DV], axis=0), (0, HEAD_IN - DV))
    gain_row = gain_row + swap(gain_row, "row")
    ends_row = jnp.pad(others[:, DV : DV + 2].reshape(-1), (0, HEAD_IN - 2 * heads))
    by_col_sums = jnp.concatenate(
        [taps.reshape(-1, HEAD_IN), gain_row[None], ends_row[None]], axis=0
    )
    by_col_sums = by_col_sums + swap(by_col_sums, "col")
    gains = jnp.concatenate([grad_gain_attn, grad_gain_mlp]).reshape(-1, HEAD_IN)
    gains = gains + swap(gains, "row")
    sums = sum_groups(jnp.concatenate([by_col_sums, gains], axis=0), groups)
    tap_rows = heads * KCONV
    grad_conv = jnp.swapaxes(
        sums[:tap_rows].reshape(heads, KCONV, HEAD_IN), 0, 1
    ).reshape(KCONV, heads * HEAD_IN)
    grad_gain_head = sums[tap_rows, :DV]
    end_pairs = sums[tap_rows + 1, : 2 * heads].reshape(heads, 2)
    gain_sums = sums[tap_rows + 2 :].reshape(2, half_width)
    return (
        result,
        input_grad,
        gain_sums[0],
        grad_w_keys,
        grad_w_values,
        grad_conv,
        end_pairs[:, 0],
        end_pairs[:, 1],
        grad_gain_head,
        grad_w_out,
        gain_sums[1],
        grad_w_gate,
        grad_w_up,
        grad_w_down,
    )


def solution(mesh):
    tokens, weights, back = P(("dp", "row"), "col"), P("col", "row"), P("row", "col")
    in_specs = (
        tokens, P("col"), weights, weights, P(None, "row"), P("row"), P("row"), P(), back,
        P("col"), weights, weights, back, P("dp", None), tokens,
    )
    out_specs = (
        tokens, tokens, P("col"), weights, weights, P(None, "row"), P("row"), P("row"), P(),
        back, P("col"), weights, weights, back,
    )
    return jax.shard_map(
        partial(layer, mesh.shape["dp"]),
        mesh=mesh,
        in_specs=in_specs,
        out_specs=out_specs,
        check_vma=False,
    )
```
